128 devices in a mesh: gx: 8 (over x_hi, z), gy: 4 (over y), gz: 4 (over x_lo, core).
Axes of the slice: x: 4 (x_hi: 2, x_lo: 2; x = x_hi * 2 + x_lo), y: 4, z: 4, core: 2. Of those that a mesh axis runs over, the one named last changes fastest.
Arguments:
- panels: bfloat16 [12288, 8192], P(('gx', 'gy'), 'gz'), may hold values from -0.75 to 0.75
- sizes: int32 [8], replicated, may hold values from 1 to 1024
- front: float32 [12288, 12288], P(('gx', 'gz'), 'gy'), may hold values from -6 to 6
Outputs:
- updated: float32 [12288, 12288], P(('gx', 'gz'), 'gy')
The draws below stay inside these ranges and needn't reach their ends.
All inputs are finite; a program needn't handle non-finite values.
Results may differ from the reference program's by a relative error of at most 0.0003.
Values may be sent and summed in bfloat16 or wider, within the bound.
A program may use at most 128 MiB of HBM per device.

```python
import jax
import jax.numpy as jnp

WIDTH = 1024
ROWS_PIECE = 384
HEIGHT = 12288
SUPER = 8
N_GX = 8
N_GY = 4


def place_ends(result, key, low, largest):
    shape = result.shape
    index_at = [jax.random.randint(jax.random.fold_in(key, axis), (), 0, shape[axis]) for axis in range(len(shape))]
    result = result.at[tuple(index_at)].set(low)
    longest = shape.index(max(shape))
    index_at[longest] = (index_at[longest] + 1) % shape[longest]
    return result.at[tuple(index_at)].set(largest)


def block_levels(rng, dims, pieces, low, top_value):
    factor_of, own = 1.0, jax.random.fold_in(rng, 6)
    for axis_at, parts in pieces:
        steps = jnp.exp(jax.random.uniform(jax.random.fold_in(own, axis_at), (parts,), jnp.float32, low / len(pieces), top_value / len(pieces)))
        factor_of = factor_of * jnp.repeat(steps, dims[axis_at] // parts).reshape([-1 if axis == axis_at else 1 for axis in range(len(dims))])
    return factor_of


def centred(rng, dims, scale, limit, cuts=(), held_as=jnp.bfloat16):
    values = jax.random.normal(rng, dims, jnp.float32) * scale
    if len(cuts) > 0:
        values = block_levels(rng, dims, cuts, -0.22, 0.18) * values
    return jnp.clip(values, min=-limit, max=limit).astype(held_as)


def setup_inputs(seed: int = 0) -> dict:
    keys = jax.random.split(jax.random.key(seed), 4)
    panels = centred(keys[0], (HEIGHT, SUPER * WIDTH), 0.125, 0.75, ((0, 32), (1, 4)))
    sizes = place_ends(jax.random.randint(keys[1], (SUPER,), 1, WIDTH + 1), jax.random.fold_in(keys[1], 1), 1, WIDTH).astype(jnp.int32)
    front = centred(keys[2], (HEIGHT, HEIGHT), 1.0, 6.0, ((0, 32), (1, 4)), jnp.float32)
    return {"panels": panels, "sizes": sizes, "front": front}


def reference(panels, sizes, front):
    column = jnp.arange(WIDTH, dtype=jnp.int32)
    live = (column[None, :] < sizes[:, None]).reshape(SUPER * WIDTH).astype(jnp.bfloat16)
    masked = panels * live[None, :]
    update = jnp.dot(masked, panels.T, preferred_element_type=jnp.float32)
    update = update.reshape(HEIGHT, N_GX, N_GY, ROWS_PIECE).transpose(0, 2, 1, 3).reshape(HEIGHT, HEIGHT)
    return front - update
```

```python
import functools

import jax
import jax.numpy as jnp
from jax import lax
from jax.experimental import pallas as pl
from jax.experimental.pallas import tpu as pltpu
from jax.sharding import PartitionSpec as P

WIDTH = 1024
PIECE = 384
HALF = PIECE // 2
CHUNK = 512
MESH = pl.DeviceIdType.MESH
Q_AT = (0, 3, 1, 2)


def device(x, y, z, c):
    return (x // 2) * 4 + z, y, (x % 2) * 2 + c


def kernel(wide, p_ref, f_ref, o_ref, cols, rows, acc, s_send, s_recv, x_send, x_recv, y_send, y_recv, l_sem, f_sem, o_sem):
    gx, y, gz = lax.axis_index("gx"), lax.axis_index("gy"), lax.axis_index("gz")
    x_lo, c, z = gz // 2, gz % 2, gx % 4
    x = (gx // 4) * 2 + x_lo
    sign = 2 * c - 1

    def at(dx, dz):
        return ((x + dx) % 4) * 4 + (z + dz) % 4

    def slot(p, s):
        return at((1 - c) * p + c * s, c * p + (1 - c) * s)

    def along_p(d):
        return device((x + (1 - c) * d) % 4, y, (z + c * d) % 4, c)

    def along_s(d):
        return device((x + c * d) % 4, y, (z + (1 - c) * d) % 4, c)

    def along_y(d):
        return device(x, (y + 4 + d * sign) % 4, z, c)

    partner = device(x, y, z, 1 - c)
    mine = p_ref.at[:, pl.ds(0, wide)]
    whole, top, bottom = pl.ds(0, PIECE), pl.ds(0, HALF), pl.ds(HALF, HALF)

    def block(core, at_slot, part=whole):
        return cols.at[core, at_slot, part]

    def send(k, src, dst, to):
        return pltpu.make_async_remote_copy(src, dst, s_send.at[k], s_recv.at[k], device_id=to, device_id_type=MESH)

    def copy(k):
        if k < 2:
            return send(k, mine, block(c, slot(0, 0)), along_p(1 + 2 * k))
        if k < 4:
            ref = block(c, slot(3 if k == 2 else 1, 0), (top, bottom)[k - 2])
            return send(k, ref, ref, along_p(2 * k - 3))
        q, kind = k // 4 - 1, k % 4
        if kind < 2:
            here = block(c, slot(Q_AT[q], 0))
            return send(k, mine if q == 0 else here, here, along_s(1 + 2 * kind))
        ref = block(c, slot(Q_AT[q], 3 if kind == 2 else 1), (top, bottom)[kind - 2])
        return send(k, ref, ref, along_s(2 * kind - 3))

    def arrival(k):
        if k < 4:
            where = (slot(3, 0), slot(1, 0), slot(2, 0), slot(2, 0))[k]
        else:
            p = Q_AT[(k - 4) // 4]
            where = (slot(p, 3), slot(p, 1), slot(p, 2), slot(p, 2))[k % 4]
        part = (whole, whole, top, bottom)[k % 4]
        ref = block(c, where, part)
        return send(k, ref, ref, partner)

    def start(*ks):
        for k in ks:
            copy(k).start()

    def take(*ks):
        for k in ks:
            arrival(k).wait_recv()

    def swap(at_slot, src=None):
        src = block(c, at_slot) if src is None else src
        return pltpu.make_async_remote_copy(
            src, block(c, at_slot), x_send.at[at_slot], x_recv.at[at_slot], device_id=partner, device_id_type=MESH
        )

    def take_swap(at_slot):
        ref = block(1 - c, at_slot)
        pltpu.make_async_remote_copy(
            ref, ref, x_send.at[at_slot], x_recv.at[at_slot], device_id=partner, device_id_type=MESH
        ).wait_recv()

    place = ((y - gz) * sign + 8) % 4
    beside = x + 1 - 2 * x_lo

    def row_src(j):
        if j == 0:
            return mine
        return block(c if j % 2 == 0 else 1 - c, (beside if j >= 2 else x) * 4 + z)

    def row_copy(j, d):
        return pltpu.make_async_remote_copy(
            row_src(j), rows.at[j], y_send.at[j, 0 if d == 1 else 1], y_recv.at[j], device_id=along_y(d), device_id_type=MESH
        )

    def row_relay(j):
        return pltpu.make_async_remote_copy(
            rows.at[j], rows.at[j], y_send.at[j, 0], y_recv.at[j], device_id=along_y(1), device_id_type=MESH
        )

    def row_local(j):
        return pltpu.make_async_copy(row_src(j), rows.at[j], l_sem.at[j])

    def row_start(j):
        @pl.when(place == 0)
        def _():
            row_copy(j, 1).start()
            row_copy(j, -1).start()
            row_local(j).start()

    def row_forward(j):
        @pl.when(place == 1)
        def _():
            row_relay(j).wait_recv()
            row_relay(j).start()

    def row_take(j):
        @pl.when(place == 0)
        def _():
            row_local(j).wait()

        @pl.when(place >= 2)
        def _():
            row_relay(j).wait_recv()

    def front(a):
        return pltpu.make_async_copy(f_ref.at[:, pl.ds(a * PIECE, PIECE)], acc.at[a], f_sem.at[a])

    def result(a):
        a_at = pl.multiple_of(a * PIECE, PIECE)
        return pltpu.make_async_copy(acc.at[a], o_ref.at[:, pl.ds(a_at, PIECE)], o_sem.at[a])

    def multiply(dx, dz, other):
        xs, zs = (x + dx) % 4, (z + dz) % 4
        a = (xs // 2) * 4 + zs
        core = c + other * (1 - 2 * c)
        j = 2 * (dx % 2) + other

        @pl.loop(0, wide // CHUNK)
        def _(i):
            at_k = pl.ds(pl.multiple_of(i * CHUNK, CHUNK), CHUNK)
            acc[a] = acc[a] - lax.dot_general(
                rows[j, :, at_k], cols[core, xs * 4 + zs, :, at_k], (((1,), (1,)), ((), ())), preferred_element_type=jnp.float32
            )

    def batch(count, offsets, fresh):
        @pl.loop(0, 2 * count)
        def _(i):
            e, other = i // 2, i % 2
            dx, dz = offsets(e)

            @pl.when((other == 1) & (e >= fresh))
            def _():
                take_swap(at(dx, dz))

            multiply(dx, dz, other)

    barrier = pltpu.get_barrier_semaphore()
    near = [along_p(1), along_p(3), along_s(1), along_s(3), along_y(1), along_y(-1), partner]
    for to in near:
        pl.semaphore_signal(barrier, inc=1, device_id=to, device_id_type=MESH)
    pl.semaphore_wait(barrier, len(near))

    here = slot(0, 0)
    start(0, 1, 4, 5)
    swap(here, mine).start()
    row_start(0)
    own = pltpu.make_async_copy(mine, block(c, here), l_sem.at[4])
    own.start()
    for a in range(8):
        front(a).start()

    take_swap(here)
    row_start(1)
    row_forward(0)

    take(0, 1)
    start(2, 3)
    take(4, 5)
    start(6, 7, 8, 9, 12, 13)
    for p, s in ((3, 0), (1, 0), (0, 3), (0, 1)):
        swap(slot(p, s)).start()
    row_start(2)
    row_forward(1)
    take_swap(at(1, 0))
    take_swap(at(3, 0))
    row_start(3)

    take(2, 3)
    start(16, 17)
    swap(slot(2, 0)).start()
    take(6, 7)
    swap(slot(0, 2)).start()
    row_forward(2)

    take(8, 9)
    start(10, 11)
    swap(slot(3, 3)).start()
    swap(slot(3, 1)).start()
    row_forward(3)
    own.wait()
    for a in range(8):
        front(a).wait()
    row_take(0)
    row_take(1)
    batch(5, lambda e: (jnp.where(e == 1, 2, 0), jnp.where(e >= 2, e - 1, 0)), 1)

    take(12, 13)
    start(14, 15)
    swap(slot(1, 3)).start()
    swap(slot(1, 1)).start()
    row_take(2)
    row_take(3)
    batch(6, lambda e: (1 + 2 * (e % 2), ((e // 2) * (e // 2 + 1)) // 2), 2)

    take(16, 17)
    start(18, 19)
    swap(slot(2, 3)).start()
    swap(slot(2, 1)).start()
    pair, other_pair = x // 2, 1 - x // 2
    early = [pair * 4 + z, pair * 4 + (z + 1) % 4, pair * 4 + (z + 3) % 4, other_pair * 4 + z]
    late = [pair * 4 + (z + 2) % 4] + [other_pair * 4 + (z + d) % 4 for d in (1, 2, 3)]
    for a in early:
        result(a).start()

    def across(p, s, other):
        turn = c + other * (1 - 2 * c)
        return (1 - turn) * p + turn * s, turn * p + (1 - turn) * s

    @pl.loop(0, 4)
    def _(i):
        e, other = i // 2, i % 2
        dx, dz = across(2, 1 + 2 * e, other)

        @pl.when(other == 1)
        def _():
            take_swap(at(dx, dz))

        multiply(dx, dz, other)

    for q in (1, 2, 3):
        k = 4 + 4 * q
        take(k + 2, k + 3)
        swap(slot(Q_AT[q], 2)).start()

        @pl.loop(0, 2)
        def _(other):
            dx, dz = across(Q_AT[q], 2, other)

            @pl.when(other == 1)
            def _():
                take_swap(at(dx, dz))

            multiply(dx, dz, other)

    for a in late:
        result(a).start()
    for k in range(20):
        copy(k).wait_send()

    @pl.loop(0, 16)
    def _(at_slot):
        swap(at_slot).wait_send()

    for j in range(4):

        @pl.when(place == 0)
        def _():
            row_copy(j, 1).wait_send()
            row_copy(j, -1).wait_send()

        @pl.when(place == 1)
        def _():
            row_relay(j).wait_send()

    for a in early + late:
        result(a).wait()


def update(panels, front, wide, number):
    call = pl.pallas_call(
        functools.partial(kernel, wide),
        out_shape=jax.ShapeDtypeStruct(front.shape, jnp.float32),
        in_specs=[pl.BlockSpec(memory_space=pl.ANY)] * 2,
        out_specs=pl.BlockSpec(memory_space=pl.ANY),
        scratch_shapes=[
            pltpu.VMEM((2, 16, PIECE, wide), jnp.bfloat16),
            pltpu.VMEM((4, PIECE, wide), jnp.bfloat16),
            pltpu.VMEM((8, PIECE, PIECE), jnp.float32),
            pltpu.SemaphoreType.DMA((20,)),
            pltpu.SemaphoreType.DMA((20,)),
            pltpu.SemaphoreType.DMA((16,)),
            pltpu.SemaphoreType.DMA((16,)),
            pltpu.SemaphoreType.DMA((4, 2)),
            pltpu.SemaphoreType.DMA((4,)),
            pltpu.SemaphoreType.DMA((5,)),
            pltpu.SemaphoreType.DMA((8,)),
            pltpu.SemaphoreType.DMA((8,)),
        ],
        compiler_params=pltpu.CompilerParams(
            collective_id=number, has_side_effects=True, vmem_limit_bytes=67043328
        ),
    )
    return call(panels, front)


def shards(panels, sizes, front):
    count = panels.shape[1] // WIDTH
    limits = lax.dynamic_slice_in_dim(sizes, lax.axis_index("gz") * count, count, 0)
    column = jnp.arange(WIDTH, dtype=jnp.int32)
    live = (column[None, :] < limits[:, None]).reshape(count * WIDTH).astype(jnp.bfloat16)
    return update(panels * live[None, :], front, count * WIDTH, 0)


def solution(mesh):
    placed = (P(("gx", "gy"), "gz"), P(), P(("gx", "gz"), "gy"))
    return jax.shard_map(
        shards, mesh=mesh, in_specs=placed, out_specs=P(("gx", "gz"), "gy"), check_vma=False
    )
```

```python
import functools

import jax
import jax.numpy as jnp
from jax import lax
from jax.experimental import pallas as pl
from jax.experimental.pallas import tpu as pltpu
from jax.sharding import PartitionSpec as P

WIDTH = 1024
PIECE = 384
HALF = PIECE // 2
LANES = 128
ROWS = 32
MESH = pl.DeviceIdType.MESH
Q_AT = (0, 3, 1, 2)
WIDES = (768, 896, 1024, 1152, 1280, 1408, 1536, 1664, 1792, 2048)


def device(x, y, z, c):
    return (x // 2) * 4 + z, y, (x % 2) * 2 + c


def kernel(wide, p_ref, f_ref, o_ref, stage, cols, rows, acc, r_send, r_recv, s_send, s_recv, x_send, x_recv, y_send, y_recv, l_sem, f_sem, o_sem):
    gx, y, gz = lax.axis_index("gx"), lax.axis_index("gy"), lax.axis_index("gz")
    x_lo, c, z = gz // 2, gz % 2, gx % 4
    x = (gx // 4) * 2 + x_lo
    sign = 2 * c - 1

    def at(dx, dz):
        return ((x + dx) % 4) * 4 + (z + dz) % 4

    def slot(p, s):
        return at((1 - c) * p + c * s, c * p + (1 - c) * s)

    def along_p(d):
        return device((x + (1 - c) * d) % 4, y, (z + c * d) % 4, c)

    def along_s(d):
        return device((x + c * d) % 4, y, (z + (1 - c) * d) % 4, c)

    def along_y(d):
        return device(x, (y + 4 + d * sign) % 4, z, c)

    partner = device(x, y, z, 1 - c)
    whole, top, bottom = pl.ds(0, PIECE), pl.ds(0, HALF), pl.ds(HALF, HALF)

    def block(core, at_slot, part=whole):
        return cols.at[core, at_slot, part]

    def send(k, src, dst, to):
        return pltpu.make_async_remote_copy(src, dst, s_send.at[k], s_recv.at[k], device_id=to, device_id_type=MESH)

    def copy(k):
        if k < 2:
            return send(k, block(c, slot(0, 0)), block(c, slot(0, 0)), along_p(1 + 2 * k))
        if k < 4:
            ref = block(c, slot(3 if k == 2 else 1, 0), (top, bottom)[k - 2])
            return send(k, ref, ref, along_p(2 * k - 3))
        q, kind = k // 4 - 1, k % 4
        if kind < 2:
            here = block(c, slot(Q_AT[q], 0))
            return send(k, here, here, along_s(1 + 2 * kind))
        ref = block(c, slot(Q_AT[q], 3 if kind == 2 else 1), (top, bottom)[kind - 2])
        return send(k, ref, ref, along_s(2 * kind - 3))

    def arrival(k):
        if k < 4:
            where = (slot(3, 0), slot(1, 0), slot(2, 0), slot(2, 0))[k]
        else:
            p = Q_AT[(k - 4) // 4]
            where = (slot(p, 3), slot(p, 1), slot(p, 2), slot(p, 2))[k % 4]
        part = (whole, whole, top, bottom)[k % 4]
        ref = block(c, where, part)
        return send(k, ref, ref, partner)

    def start(*ks):
        for k in ks:
            copy(k).start()

    def take(*ks):
        for k in ks:
            arrival(k).wait_recv()

    def swap(at_slot):
        src = block(c, at_slot)
        return pltpu.make_async_remote_copy(
            src, block(c, at_slot), x_send.at[at_slot], x_recv.at[at_slot], device_id=partner, device_id_type=MESH
        )

    def take_swap(at_slot):
        ref = block(1 - c, at_slot)
        pltpu.make_async_remote_copy(
            ref, ref, x_send.at[at_slot], x_recv.at[at_slot], device_id=partner, device_id_type=MESH
        ).wait_recv()

    place = ((y - gz) * sign + 8) % 4
    beside = x + 1 - 2 * x_lo

    def row_src(j):
        return block(c if j % 2 == 0 else 1 - c, (beside if j >= 2 else x) * 4 + z)

    def row_copy(j, d):
        return pltpu.make_async_remote_copy(
            row_src(j), rows.at[j], y_send.at[j, 0 if d == 1 else 1], y_recv.at[j], device_id=along_y(d), device_id_type=MESH
        )

    def row_relay(j):
        return pltpu.make_async_remote_copy(
            rows.at[j], rows.at[j], y_send.at[j, 0], y_recv.at[j], device_id=along_y(1), device_id_type=MESH
        )

    def row_local(j):
        return pltpu.make_async_copy(row_src(j), rows.at[j], l_sem.at[j])

    def row_start(j):
        @pl.when(place == 0)
        def _():
            row_copy(j, 1).start()
            row_copy(j, -1).start()
            row_local(j).start()

    def row_forward(j):
        @pl.when(place == 1)
        def _():
            row_relay(j).wait_recv()
            row_relay(j).start()

    def row_take(j):
        @pl.when(place == 0)
        def _():
            row_local(j).wait()

        @pl.when(place >= 2)
        def _():
            row_relay(j).wait_recv()

    def front(a):
        return pltpu.make_async_copy(f_ref.at[:, pl.ds(a * PIECE, PIECE)], acc.at[a], f_sem.at[a])

    def result(a):
        a_at = pl.multiple_of(a * PIECE, PIECE)
        return pltpu.make_async_copy(acc.at[a], o_ref.at[:, pl.ds(a_at, PIECE)], o_sem.at[a])

    def multiply(dx, dz, other):
        xs, zs = (x + dx) % 4, (z + dz) % 4
        a = (xs // 2) * 4 + zs
        core = c + other * (1 - 2 * c)
        j = 2 * (dx % 2) + other

        acc[a] = acc[a] - lax.dot_general(
            rows[j], cols[core, xs * 4 + zs], (((1,), (1,)), ((), ())), preferred_element_type=jnp.float32
        )

    here = slot(0, 0)

    own = pltpu.make_async_copy(p_ref.at[:, pl.ds(pl.multiple_of(c * wide, LANES), wide)], block(c, here), l_sem.at[4])
    own.start()
    for a in range(8):
        front(a).start()
    barrier = pltpu.get_barrier_semaphore()
    near = [along_p(1), along_p(3), along_s(1), along_s(3), along_y(1), along_y(-1), partner]
    for to in near:
        pl.semaphore_signal(barrier, inc=1, device_id=to, device_id_type=MESH)
    pl.semaphore_wait(barrier, len(near))

    share = pltpu.make_async_remote_copy(
        p_ref.at[:, pl.ds(pl.multiple_of((1 - c) * wide, LANES), wide)],
        stage,
        r_send,
        r_recv,
        device_id=partner,
        device_id_type=MESH,
    )
    share.start()
    own.wait()
    share.wait_recv()

    @pl.loop(0, PIECE // ROWS)
    def _(i):
        at_rows = pl.ds(pl.multiple_of(i * ROWS, ROWS), ROWS)
        cols[c, here, at_rows] = cols[c, here, at_rows] + stage[at_rows]

    start(0, 1, 4, 5)
    swap(here).start()
    row_start(0)

    take_swap(here)
    row_start(1)
    row_forward(0)

    take(0, 1)
    start(2, 3)
    take(4, 5)
    start(6, 7, 8, 9, 12, 13)
    for p, s in ((3, 0), (1, 0), (0, 3), (0, 1)):
        swap(slot(p, s)).start()
    row_start(2)
    row_forward(1)
    take_swap(at(1, 0))
    take_swap(at(3, 0))
    row_start(3)

    take(2, 3)
    start(16, 17)
    swap(slot(2, 0)).start()
    take(6, 7)
    swap(slot(0, 2)).start()
    row_forward(2)

    take(8, 9)
    start(10, 11)
    swap(slot(3, 3)).start()
    swap(slot(3, 1)).start()
    row_forward(3)
    for a in range(8):
        front(a).wait()
    row_take(0)
    row_take(1)
    pair, other_pair = x // 2, 1 - x // 2
    early = [pair * 4 + z, pair * 4 + (z + 1) % 4, pair * 4 + (z + 3) % 4, other_pair * 4 + z]
    late = [pair * 4 + (z + 2) % 4] + [other_pair * 4 + (z + d) % 4 for d in (1, 2, 3)]

    @pl.loop(0, 32)
    def _(i):
        @pl.when(i == 10)
        def _():
            take(12, 13)
            start(14, 15)
            swap(slot(1, 3)).start()
            swap(slot(1, 1)).start()
            row_take(2)
            row_take(3)

        @pl.when(i == 22)
        def _():
            take(16, 17)
            start(18, 19)
            swap(slot(2, 3)).start()
            swap(slot(2, 1)).start()
            for a in early:
                result(a).start()

        for q in (1, 2, 3):

            @pl.when(i == 24 + 2 * q)
            def _():
                take(6 + 4 * q, 7 + 4 * q)
                swap(slot(Q_AT[q], 2)).start()

        other = i % 2
        e, f, g, h = i // 2, i // 2 - 5, i // 2 - 11, i // 2 - 13
        ahead = jnp.where(i < 26, 2, jnp.where(h == 0, 3, h))
        aside = jnp.where(i < 26, 1 + 2 * g, 2)
        turn = c + other * (1 - 2 * c)
        late_x, late_z = (1 - turn) * ahead + turn * aside, turn * ahead + (1 - turn) * aside
        near_x, near_z = jnp.where(e == 1, 2, 0), jnp.where(e >= 2, e - 1, 0)
        next_x, next_z = 1 + 2 * (f % 2), (f // 2) * (f // 2 + 1) // 2
        dx = jnp.where(i < 10, near_x, jnp.where(i < 22, next_x, late_x))
        dz = jnp.where(i < 10, near_z, jnp.where(i < 22, next_z, late_z))

        @pl.when((other == 1) & (i != 1) & (i != 11) & (i != 13))
        def _():
            take_swap(at(dx, dz))

        multiply(dx, dz, other)

    for a in late:
        result(a).start()
    share.wait_send()
    for k in range(20):
        copy(k).wait_send()

    @pl.loop(0, 16)
    def _(at_slot):
        swap(at_slot).wait_send()

    for j in range(4):

        @pl.when(place == 0)
        def _():
            row_copy(j, 1).wait_send()
            row_copy(j, -1).wait_send()

        @pl.when(place == 1)
        def _():
            row_relay(j).wait_send()

    for a in early + late:
        result(a).wait()


def pack(sizes_ref, p_ref, o_ref, branch_ref):
    gz = lax.axis_index("gz")
    totals = [sum(sizes_ref[4 * k + i] for i in range(4)) for k in range(2)]
    need = (jnp.maximum(totals[0], totals[1]) + 1) // 2
    branch, wide = 0, WIDES[0]
    for low, high in zip(WIDES[:-1], WIDES[1:]):
        over = (need > low).astype(jnp.int32)
        branch, wide = branch + over, wide + over * (high - low)
    branch_ref[0] = branch
    sizes = [sizes_ref[2 * gz], sizes_ref[2 * gz + 1]]
    begin = (gz % 2) * (2 * wide - sizes[0] - sizes[1])
    begins = [begin, begin + sizes[0], begin + sizes[0] + sizes[1]]
    shift = lax.broadcasted_iota(jnp.int32, (2 * LANES, LANES), 0) - lax.broadcasted_iota(jnp.int32, (2 * LANES, LANES), 1)
    lane = lax.broadcasted_iota(jnp.int32, (2 * LANES, LANES), 1)

    @pl.loop(0, 2 * wide // LANES)
    def _(t):
        first = t * LANES
        here = pl.ds(pl.multiple_of(first, LANES), LANES)
        used = (first < begins[2]) & (first + LANES > begins[0])

        @pl.when(used)
        def _():
            total = jnp.zeros((PIECE, LANES), jnp.float32)
            for k in range(2):
                ahead = first - begins[k]
                window = jnp.clip((ahead + 4 * WIDTH) // LANES * LANES - 4 * WIDTH, 0, WIDTH - 2 * LANES)
                pick = (shift == ahead - window) & (lane < begins[k + 1] - first)
                part = p_ref[:, pl.ds(pl.multiple_of(k * WIDTH + window, LANES), 2 * LANES)]
                total += jnp.dot(part, pick.astype(jnp.bfloat16), preferred_element_type=jnp.float32)
            o_ref[:, here] = total.astype(jnp.bfloat16)

        @pl.when(jnp.logical_not(used))
        def _():
            o_ref[:, here] = jnp.zeros((PIECE, LANES), jnp.bfloat16)


def update(wide, number, packed, front):
    call = pl.pallas_call(
        functools.partial(kernel, wide),
        out_shape=jax.ShapeDtypeStruct(front.shape, jnp.float32),
        in_specs=[pl.BlockSpec(memory_space=pl.ANY)] * 2,
        out_specs=pl.BlockSpec(memory_space=pl.ANY),
        scratch_shapes=[
            pltpu.VMEM((PIECE, wide), jnp.bfloat16),
            pltpu.VMEM((2, 16, PIECE, wide), jnp.bfloat16),
            pltpu.VMEM((4, PIECE, wide), jnp.bfloat16),
            pltpu.VMEM((8, PIECE, PIECE), jnp.float32),
            pltpu.SemaphoreType.DMA,
            pltpu.SemaphoreType.DMA,
            pltpu.SemaphoreType.DMA((20,)),
            pltpu.SemaphoreType.DMA((20,)),
            pltpu.SemaphoreType.DMA((16,)),
            pltpu.SemaphoreType.DMA((16,)),
            pltpu.SemaphoreType.DMA((4, 2)),
            pltpu.SemaphoreType.DMA((4,)),
            pltpu.SemaphoreType.DMA((5,)),
            pltpu.SemaphoreType.DMA((8,)),
            pltpu.SemaphoreType.DMA((8,)),
        ],
        compiler_params=pltpu.CompilerParams(
            collective_id=number, has_side_effects=True, vmem_limit_bytes=67043328
        ),
    )
    return call(packed, front)


def shards(panels, sizes, front):
    packed, branch = pl.pallas_call(
        pack,
        out_shape=[
            jax.ShapeDtypeStruct((PIECE, 4 * WIDTH), jnp.bfloat16),
            jax.ShapeDtypeStruct((1,), jnp.int32),
        ],
        in_specs=[pl.BlockSpec(memory_space=pltpu.SMEM), pl.BlockSpec(memory_space=pltpu.VMEM)],
        out_specs=[pl.BlockSpec(memory_space=pltpu.VMEM), pl.BlockSpec(memory_space=pltpu.SMEM)],
    )(sizes, panels)
    calls = [functools.partial(update, wide, number) for number, wide in enumerate(WIDES)]
    return lax.switch(branch[0], calls, packed, front)


def solution(mesh):
    placed = (P(("gx", "gy"), "gz"), P(), P(("gx", "gz"), "gy"))
    return jax.shard_map(
        shards, mesh=mesh, in_specs=placed, out_specs=P(("gx", "gz"), "gy"), check_vma=False
    )
```

```python
import functools

import jax
import jax.numpy as jnp
from jax import lax
from jax.experimental import pallas as pl
from jax.experimental.pallas import tpu as pltpu
from jax.sharding import PartitionSpec as P

WIDTH = 1024
PIECE = 384
HALF = PIECE // 2
LANES = 128
ROWS = 32
TILE = 256
WINDOW = TILE + LANES
MESH = pl.DeviceIdType.MESH
Q_AT = (0, 3, 1, 2)
WIDES = (640, 768, 896, 1024, 1152, 1280, 1408, 1536, 1792, 2048)
EXTRA = 256


def device(x, y, z, c):
    return (x // 2) * 4 + z, y, (x % 2) * 2 + c


def kernel(wide, p_ref, f_ref, acc, stage, over, taken, cols, rows, r_send, r_recv, i_send, i_recv, s_send, s_recv, x_send, x_recv, y_send, y_recv, l_sem, f_sem):
    gx, y, gz = lax.axis_index("gx"), lax.axis_index("gy"), lax.axis_index("gz")
    x_lo, c, z = gz // 2, gz % 2, gx % 4
    x = (gx // 4) * 2 + x_lo
    sign = 2 * c - 1

    def at(dx, dz):
        return ((x + dx) % 4) * 4 + (z + dz) % 4

    def slot(p, s):
        return at((1 - c) * p + c * s, c * p + (1 - c) * s)

    def along_p(d):
        return device((x + (1 - c) * d) % 4, y, (z + c * d) % 4, c)

    def along_s(d):
        return device((x + c * d) % 4, y, (z + (1 - c) * d) % 4, c)

    def along_y(d):
        return device(x, (y + 4 + d * sign) % 4, z, c)

    partner = device(x, y, z, 1 - c)
    whole, top, bottom = pl.ds(0, PIECE), pl.ds(0, HALF), pl.ds(HALF, HALF)

    def block(core, at_slot, part=whole):
        return cols.at[core, at_slot, part]

    def send(k, src, dst, to):
        return pltpu.make_async_remote_copy(src, dst, s_send.at[k], s_recv.at[k], device_id=to, device_id_type=MESH)

    def copy(k):
        if k < 2:
            return send(k, block(c, slot(0, 0)), block(c, slot(0, 0)), along_p(1 + 2 * k))
        if k < 4:
            ref = block(c, slot(3 if k == 2 else 1, 0), (top, bottom)[k - 2])
            return send(k, ref, ref, along_p(2 * k - 3))
        q, kind = k // 4 - 1, k % 4
        if kind < 2:
            here = block(c, slot(Q_AT[q], 0))
            return send(k, here, here, along_s(1 + 2 * kind))
        ref = block(c, slot(Q_AT[q], 3 if kind == 2 else 1), (top, bottom)[kind - 2])
        return send(k, ref, ref, along_s(2 * kind - 3))

    def arrival(k):
        if k < 4:
            where = (slot(3, 0), slot(1, 0), slot(2, 0), slot(2, 0))[k]
        else:
            p = Q_AT[(k - 4) // 4]
            where = (slot(p, 3), slot(p, 1), slot(p, 2), slot(p, 2))[k % 4]
        part = (whole, whole, top, bottom)[k % 4]
        ref = block(c, where, part)
        return send(k, ref, ref, partner)

    def start(*ks):
        for k in ks:
            copy(k).start()

    def take(*ks):
        for k in ks:
            arrival(k).wait_recv()

    def swap(at_slot):
        src = block(c, at_slot)
        return pltpu.make_async_remote_copy(
            src, block(c, at_slot), x_send.at[at_slot], x_recv.at[at_slot], device_id=partner, device_id_type=MESH
        )

    def take_swap(at_slot):
        ref = block(1 - c, at_slot)
        pltpu.make_async_remote_copy(
            ref, ref, x_send.at[at_slot], x_recv.at[at_slot], device_id=partner, device_id_type=MESH
        ).wait_recv()

    place = ((y - gz) * sign + 8) % 4
    beside = x + 1 - 2 * x_lo

    def row_src(j):
        return block(c if j % 2 == 0 else 1 - c, (beside if j >= 2 else x) * 4 + z)

    def row_copy(j, d):
        return pltpu.make_async_remote_copy(
            row_src(j), rows.at[j], y_send.at[j, 0 if d == 1 else 1], y_recv.at[j], device_id=along_y(d), device_id_type=MESH
        )

    def row_relay(j):
        return pltpu.make_async_remote_copy(
            rows.at[j], rows.at[j], y_send.at[j, 0], y_recv.at[j], device_id=along_y(1), device_id_type=MESH
        )

    def row_local(j):
        return pltpu.make_async_copy(row_src(j), rows.at[j], l_sem.at[j])

    def row_start(j):
        @pl.when(place == 0)
        def _():
            row_copy(j, 1).start()
            row_copy(j, -1).start()
            row_local(j).start()

    def row_forward(j):
        @pl.when(place == 1)
        def _():
            row_relay(j).wait_recv()
            row_relay(j).start()

    def row_take(j):
        @pl.when(place == 0)
        def _():
            row_local(j).wait()

        @pl.when(place >= 2)
        def _():
            row_relay(j).wait_recv()

    def front(a):
        return pltpu.make_async_copy(f_ref.at[:, pl.ds(a * PIECE, PIECE)], acc.at[a], f_sem.at[a])

    def multiply(dx, dz, other):
        xs, zs = (x + dx) % 4, (z + dz) % 4
        a = (xs // 2) * 4 + zs
        core = c + other * (1 - 2 * c)
        j = 2 * (dx % 2) + other

        acc[a] = acc[a] - lax.dot_general(
            rows[j], cols[core, xs * 4 + zs], (((1,), (1,)), ((), ())), preferred_element_type=jnp.float32
        )

    here = slot(0, 0)

    extra = 0 if wide == 2 * WIDTH else EXTRA
    mine_at, other_at = (x_lo + c) % 2 * wide, (x_lo + c + 1) % 2 * wide
    block_in, over_in = x_lo * extra, (1 - x_lo) * wide

    def columns(begin, count):
        return pl.ds(pl.multiple_of(begin, LANES), count)

    own = pltpu.make_async_copy(p_ref.at[:, columns(mine_at + block_in, wide)], block(c, here), l_sem.at[4])
    own.start()
    for a in range(8):
        front(a).start()
    barrier = pltpu.get_barrier_semaphore()
    near = [along_p(1), along_p(3), along_s(1), along_s(3), along_y(1), along_y(-1), partner]
    for to in near:
        pl.semaphore_signal(barrier, inc=1, device_id=to, device_id_type=MESH)
    pl.semaphore_wait(barrier, len(near))

    share = pltpu.make_async_remote_copy(
        p_ref.at[:, columns(other_at, wide + extra)], stage, r_send, r_recv, device_id=partner, device_id_type=MESH
    )
    share.start()
    if extra:
        give = pltpu.make_async_remote_copy(
            over, taken, i_send, i_recv, device_id=device(beside, y, z, c), device_id_type=MESH
        )
        spare = pltpu.make_async_copy(p_ref.at[:, columns(mine_at + over_in, extra)], over, l_sem.at[5])
        spare.start()
        spare.wait()
    own.wait()
    share.wait_recv()
    if extra:

        @pl.when(c == 1)
        def _():
            over[...] = over[...] + stage[:, columns(over_in, extra)]
            give.start()

    @pl.loop(0, PIECE // ROWS)
    def _(i):
        at_rows = pl.ds(pl.multiple_of(i * ROWS, ROWS), ROWS)
        cols[c, here, at_rows] = cols[c, here, at_rows] + stage[at_rows, columns(block_in, wide)]

    if extra:

        @pl.when(c == 1)
        def _():
            give.wait_recv()
            took = columns((1 - x_lo) * (wide - extra), extra)
            cols[c, here, :, took] = cols[c, here, :, took] + taken[...]

    start(0, 1, 4, 5)
    swap(here).start()
    row_start(0)

    take_swap(here)
    row_start(1)
    row_forward(0)

    take(0, 1)
    start(2, 3)
    take(4, 5)
    start(6, 7, 8, 9, 12, 13)
    for p, s in ((3, 0), (1, 0), (0, 3), (0, 1)):
        swap(slot(p, s)).start()
    row_start(2)
    row_forward(1)
    take_swap(at(1, 0))
    take_swap(at(3, 0))
    row_start(3)

    take(2, 3)
    start(16, 17)
    swap(slot(2, 0)).start()
    take(6, 7)
    swap(slot(0, 2)).start()
    row_forward(2)

    take(8, 9)
    start(10, 11)
    swap(slot(3, 3)).start()
    swap(slot(3, 1)).start()
    row_forward(3)
    for a in range(8):
        front(a).wait()
    row_take(0)
    row_take(1)

    @pl.loop(0, 32)
    def _(i):
        @pl.when(i == 10)
        def _():
            take(12, 13)
            start(14, 15)
            swap(slot(1, 3)).start()
            swap(slot(1, 1)).start()
            row_take(2)
            row_take(3)

        @pl.when(i == 22)
        def _():
            take(16, 17)
            start(18, 19)
            swap(slot(2, 3)).start()
            swap(slot(2, 1)).start()

        for q in (1, 2, 3):

            @pl.when(i == 24 + 2 * q)
            def _():
                take(6 + 4 * q, 7 + 4 * q)
                swap(slot(Q_AT[q], 2)).start()

        other = i % 2
        e, f, g, h = i // 2, i // 2 - 5, i // 2 - 11, i // 2 - 13
        ahead = jnp.where(i < 26, 2, jnp.where(h == 0, 3, h))
        aside = jnp.where(i < 26, 1 + 2 * g, 2)
        turn = c + other * (1 - 2 * c)
        late_x, late_z = (1 - turn) * ahead + turn * aside, turn * ahead + (1 - turn) * aside
        near_x, near_z = jnp.where(e == 1, 2, 0), jnp.where(e >= 2, e - 1, 0)
        next_x, next_z = 1 + 2 * (f % 2), (f // 2) * (f // 2 + 1) // 2
        dx = jnp.where(i < 10, near_x, jnp.where(i < 22, next_x, late_x))
        dz = jnp.where(i < 10, near_z, jnp.where(i < 22, next_z, late_z))

        @pl.when((other == 1) & (i != 1) & (i != 11) & (i != 13))
        def _():
            take_swap(at(dx, dz))

        multiply(dx, dz, other)

    share.wait_send()
    if extra:

        @pl.when(c == 1)
        def _():
            give.wait_send()

    for k in range(20):
        copy(k).wait_send()

    @pl.loop(0, 16)
    def _(at_slot):
        swap(at_slot).wait_send()

    for j in range(4):

        @pl.when(place == 0)
        def _():
            row_copy(j, 1).wait_send()
            row_copy(j, -1).wait_send()

        @pl.when(place == 1)
        def _():
            row_relay(j).wait_send()


def pack(sizes_ref, p_ref, o_ref, branch_ref, panel, sem):
    gz = lax.axis_index("gz")
    fetches = []
    for k in range(2):
        part = pl.ds(k * WIDTH, WIDTH)
        fetches.append(pltpu.make_async_copy(p_ref.at[:, part], panel.at[:, part], sem.at[k]))
        fetches[k].start()
    totals = [sum(sizes_ref[4 * k + i] for i in range(4)) for k in range(2)]
    need = jnp.maximum((jnp.maximum(totals[0], totals[1]) + 1 - EXTRA) // 2, (totals[0] + totals[1] + 3) // 4)
    branch, wide = 0, WIDES[0]
    for low, high in zip(WIDES[:-1], WIDES[1:]):
        over = (need > low).astype(jnp.int32)
        branch, wide = branch + over, wide + over * (high - low)
    branch_ref[0] = branch
    extra = EXTRA * (need <= WIDES[-2]).astype(jnp.int32)
    end = 2 * wide + extra
    sizes = [sizes_ref[2 * gz], sizes_ref[2 * gz + 1]]
    begin = jnp.where(gz == 0, 0, jnp.where(gz == 1, totals[0], end)) - jnp.where(gz == 3, totals[1], jnp.where(gz == 0, 0, sizes[0] + sizes[1]))
    begins = [begin, begin + sizes[0], begin + sizes[0] + sizes[1]]
    shift = lax.broadcasted_iota(jnp.int32, (WINDOW, TILE), 0) - lax.broadcasted_iota(jnp.int32, (WINDOW, TILE), 1)
    lane = lax.broadcasted_iota(jnp.int32, (WINDOW, TILE), 1)

    @pl.loop(0, end // TILE)
    def _(t):
        o_ref[:, pl.ds(pl.multiple_of(t * TILE, TILE), TILE)] = jnp.zeros((PIECE, TILE), jnp.bfloat16)

    for k in range(2):
        fetches[k].wait()

        def place(t, carry):
            ahead = t * TILE - begins[k]
            window = jnp.clip((ahead + 4 * WIDTH) // LANES * LANES - 4 * WIDTH, 0, WIDTH - WINDOW)
            pick = (shift == ahead - window) & (lane < begins[k + 1] - t * TILE)
            part = panel[:, pl.ds(pl.multiple_of(k * WIDTH + window, LANES), WINDOW)]
            moved = jnp.dot(part, pick.astype(jnp.bfloat16), preferred_element_type=jnp.float32).astype(jnp.bfloat16)
            here = pl.ds(pl.multiple_of(t * TILE, TILE), TILE)
            o_ref[:, here] = o_ref[:, here] + moved
            return carry

        lax.fori_loop(begins[k] // TILE, (begins[k + 1] + TILE - 1) // TILE, place, 0)


def deliver(acc, o_ref, sem):
    moves = [pltpu.make_async_copy(acc.at[a], o_ref.at[:, pl.ds(a * PIECE, PIECE)], sem.at[a]) for a in range(8)]
    for move in moves:
        move.start()
    for move in moves:
        move.wait()


def update(wide, number, packed, front):
    extra = 0 if wide == 2 * WIDTH else EXTRA
    call = pl.pallas_call(
        functools.partial(kernel, wide),
        out_shape=pltpu.VMEM((8, PIECE, PIECE), jnp.float32),
        in_specs=[pl.BlockSpec(memory_space=pl.ANY)] * 2,
        out_specs=pl.BlockSpec(memory_space=pltpu.VMEM),
        scratch_shapes=[
            pltpu.VMEM((PIECE, wide + extra), jnp.bfloat16),
            pltpu.VMEM((PIECE, max(extra, LANES)), jnp.bfloat16),
            pltpu.VMEM((PIECE, max(extra, LANES)), jnp.bfloat16),
            pltpu.VMEM((2, 16, PIECE, wide), jnp.bfloat16),
            pltpu.VMEM((4, PIECE, wide), jnp.bfloat16),
            pltpu.SemaphoreType.DMA,
            pltpu.SemaphoreType.DMA,
            pltpu.SemaphoreType.DMA,
            pltpu.SemaphoreType.DMA,
            pltpu.SemaphoreType.DMA((20,)),
            pltpu.SemaphoreType.DMA((20,)),
            pltpu.SemaphoreType.DMA((16,)),
            pltpu.SemaphoreType.DMA((16,)),
            pltpu.SemaphoreType.DMA((4, 2)),
            pltpu.SemaphoreType.DMA((4,)),
            pltpu.SemaphoreType.DMA((6,)),
            pltpu.SemaphoreType.DMA((8,)),
        ],
        compiler_params=pltpu.CompilerParams(
            collective_id=number, has_side_effects=True, vmem_limit_bytes=PIECE * 2 * (37 * wide + 3 * max(extra, LANES)) + (2**20 if wide == 2 * WIDTH else 2**21)
        ),
    )
    return pl.pallas_call(
        deliver,
        out_shape=jax.ShapeDtypeStruct(front.shape, jnp.float32),
        in_specs=[pl.BlockSpec(memory_space=pltpu.VMEM)],
        out_specs=pl.BlockSpec(memory_space=pl.ANY),
        scratch_shapes=[pltpu.SemaphoreType.DMA((8,))],
        compiler_params=pltpu.CompilerParams(vmem_limit_bytes=2**20),
    )(call(packed, front))


def shards(panels, sizes, front):
    packed, branch = pl.pallas_call(
        pack,
        out_shape=[
            jax.ShapeDtypeStruct((PIECE, 4 * WIDTH), jnp.bfloat16),
            jax.ShapeDtypeStruct((1,), jnp.int32),
        ],
        in_specs=[pl.BlockSpec(memory_space=pltpu.SMEM), pl.BlockSpec(memory_space=pl.ANY)],
        out_specs=[pl.BlockSpec(memory_space=pltpu.VMEM), pl.BlockSpec(memory_space=pltpu.SMEM)],
        scratch_shapes=[pltpu.VMEM((PIECE, 2 * WIDTH), jnp.bfloat16), pltpu.SemaphoreType.DMA((2,))],
    )(sizes, panels)
    calls = [functools.partial(update, wide, number) for number, wide in enumerate(WIDES)]
    return lax.switch(branch[0], calls, packed, front)


def solution(mesh):
    placed = (P(("gx", "gy"), "gz"), P(), P(("gx", "gz"), "gy"))
    return jax.shard_map(
        shards, mesh=mesh, in_specs=placed, out_specs=P(("gx", "gz"), "gy"), check_vma=False
    )
```

```python
import functools

import jax
import jax.numpy as jnp
from jax import lax
from jax.experimental import pallas as pl
from jax.experimental.pallas import tpu as pltpu
from jax.sharding import PartitionSpec as P

WIDTH = 1024
PIECE = 384
LANES = 128
STEP = 64
TILE = 256
WINDOW = TILE + LANES
MESH = pl.DeviceIdType.MESH
Q_AT = (0, 3, 1, 2)
WIDES = (704, 832, 896, 960, 1024, 1088, 1152, 1216, 1280, 1344, 1408, 1536, 1792, 2048)
EXTRA = 256


def device(x, y, z, c):
    return (x // 2) * 4 + z, y, (x % 2) * 2 + c


def kernel(wide, p_ref, f_ref, acc, stage, over, taken, cols, rows, r_send, r_recv, i_send, i_recv, s_send, s_recv, x_send, x_recv, y_send, y_recv, l_sem, f_sem):
    gx, y, gz = lax.axis_index("gx"), lax.axis_index("gy"), lax.axis_index("gz")
    x_lo, c, z = gz // 2, gz % 2, gx % 4
    x = (gx // 4) * 2 + x_lo
    sign = 2 * c - 1

    def at(dx, dz):
        return ((x + dx) % 4) * 4 + (z + dz) % 4

    def slot(p, s):
        return at((1 - c) * p + c * s, c * p + (1 - c) * s)

    def along_p(d):
        return device((x + (1 - c) * d) % 4, y, (z + c * d) % 4, c)

    def along_s(d):
        return device((x + c * d) % 4, y, (z + (1 - c) * d) % 4, c)

    def along_y(d):
        return device(x, (y + 4 + d * sign) % 4, z, c)

    partner = device(x, y, z, 1 - c)
    whole, top, bottom = pl.ds(0, wide), pl.ds(0, wide // 2), pl.ds(wide // 2, wide // 2)

    def block(core, at_slot, part=whole):
        return cols.at[core, at_slot, part]

    def send(k, src, dst, to):
        return pltpu.make_async_remote_copy(src, dst, s_send.at[k], s_recv.at[k], device_id=to, device_id_type=MESH)

    def copy(k):
        if k < 2:
            return send(k, block(c, slot(0, 0)), block(c, slot(0, 0)), along_p(1 + 2 * k))
        if k < 4:
            ref = block(c, slot(3 if k == 2 else 1, 0), (top, bottom)[k - 2])
            return send(k, ref, ref, along_p(2 * k - 3))
        q, kind = k // 4 - 1, k % 4
        if kind < 2:
            here = block(c, slot(Q_AT[q], 0))
            return send(k, here, here, along_s(1 + 2 * kind))
        ref = block(c, slot(Q_AT[q], 3 if kind == 2 else 1), (top, bottom)[kind - 2])
        return send(k, ref, ref, along_s(2 * kind - 3))

    def arrival(k):
        if k < 4:
            where = (slot(3, 0), slot(1, 0), slot(2, 0), slot(2, 0))[k]
        else:
            p = Q_AT[(k - 4) // 4]
            where = (slot(p, 3), slot(p, 1), slot(p, 2), slot(p, 2))[k % 4]
        part = (whole, whole, top, bottom)[k % 4]
        ref = block(c, where, part)
        return send(k, ref, ref, partner)

    def start(*ks):
        for k in ks:
            copy(k).start()

    def take(*ks):
        for k in ks:
            arrival(k).wait_recv()

    def swap(at_slot):
        src = block(c, at_slot)
        return pltpu.make_async_remote_copy(
            src, block(c, at_slot), x_send.at[at_slot], x_recv.at[at_slot], device_id=partner, device_id_type=MESH
        )

    def take_swap(at_slot):
        ref = block(1 - c, at_slot)
        pltpu.make_async_remote_copy(
            ref, ref, x_send.at[at_slot], x_recv.at[at_slot], device_id=partner, device_id_type=MESH
        ).wait_recv()

    place = ((y - gz) * sign + 8) % 4
    beside = x + 1 - 2 * x_lo

    def row_src(j):
        return block(c if j % 2 == 0 else 1 - c, (beside if j >= 2 else x) * 4 + z)

    def row_copy(j, d):
        return pltpu.make_async_remote_copy(
            row_src(j), rows.at[j], y_send.at[j, 0 if d == 1 else 1], y_recv.at[j], device_id=along_y(d), device_id_type=MESH
        )

    def row_relay(j):
        return pltpu.make_async_remote_copy(
            rows.at[j], rows.at[j], y_send.at[j, 0], y_recv.at[j], device_id=along_y(1), device_id_type=MESH
        )

    def row_local(j):
        return pltpu.make_async_copy(row_src(j), rows.at[j], l_sem.at[j])

    def row_start(j):
        @pl.when(place == 0)
        def _():
            row_copy(j, 1).start()
            row_copy(j, -1).start()
            row_local(j).start()

    def row_forward(j):
        @pl.when(place == 1)
        def _():
            row_relay(j).wait_recv()
            row_relay(j).start()

    def row_take(j):
        @pl.when(place == 0)
        def _():
            row_local(j).wait()

        @pl.when(place >= 2)
        def _():
            row_relay(j).wait_recv()

    def front(a):
        return pltpu.make_async_copy(f_ref.at[:, pl.ds(a * PIECE, PIECE)], acc.at[a], f_sem.at[a])

    def multiply(dx, dz, other):
        xs, zs = (x + dx) % 4, (z + dz) % 4
        a = (xs // 2) * 4 + zs
        core = c + other * (1 - 2 * c)
        j = 2 * (dx % 2) + other

        acc[a] = acc[a] - lax.dot_general(
            rows[j], cols[core, xs * 4 + zs], (((0,), (0,)), ((), ())), preferred_element_type=jnp.float32
        )

    here = slot(0, 0)

    extra = 0 if wide == 2 * WIDTH else EXTRA
    mine_at, other_at = (x_lo + c) % 2 * wide, (x_lo + c + 1) % 2 * wide
    block_in, over_in = x_lo * extra, (1 - x_lo) * wide

    def columns(begin, count):
        return pl.ds(pl.multiple_of(begin, STEP), count)

    own = pltpu.make_async_copy(p_ref.at[columns(mine_at + block_in, wide)], block(c, here), l_sem.at[4])
    own.start()
    for a in range(8):
        front(a).start()
    barrier = pltpu.get_barrier_semaphore()
    near = [along_p(1), along_p(3), along_s(1), along_s(3), along_y(1), along_y(-1), partner]
    for to in near:
        pl.semaphore_signal(barrier, inc=1, device_id=to, device_id_type=MESH)
    pl.semaphore_wait(barrier, len(near))

    share = pltpu.make_async_remote_copy(
        p_ref.at[columns(other_at, wide + extra)], stage, r_send, r_recv, device_id=partner, device_id_type=MESH
    )
    share.start()
    if extra:
        give = pltpu.make_async_remote_copy(
            over, taken, i_send, i_recv, device_id=device(beside, y, z, c), device_id_type=MESH
        )
        spare = pltpu.make_async_copy(p_ref.at[columns(mine_at + over_in, extra)], over, l_sem.at[5])
        spare.start()
        spare.wait()
    own.wait()
    share.wait_recv()
    if extra:

        @pl.when(c == 1)
        def _():
            over[...] = over[...] + stage[columns(over_in, extra)]
            give.start()

    @pl.loop(0, wide // STEP)
    def _(i):
        at_rows = columns(i * STEP, STEP)
        cols[c, here, at_rows] = cols[c, here, at_rows] + stage[columns(block_in + i * STEP, STEP)]

    if extra:

        @pl.when(c == 1)
        def _():
            give.wait_recv()
            took = columns((1 - x_lo) * (wide - extra), extra)
            cols[c, here, took] = cols[c, here, took] + taken[...]

    start(0, 1, 4, 5)
    swap(here).start()
    row_start(0)

    take_swap(here)
    row_start(1)
    row_forward(0)

    take(0, 1)
    start(2, 3)
    take(4, 5)
    start(6, 7, 8, 9, 12, 13)
    for p, s in ((3, 0), (1, 0), (0, 3), (0, 1)):
        swap(slot(p, s)).start()
    row_start(2)
    row_forward(1)
    take_swap(at(1, 0))
    take_swap(at(3, 0))
    row_start(3)

    take(2, 3)
    start(16, 17)
    swap(slot(2, 0)).start()
    take(6, 7)
    swap(slot(0, 2)).start()
    row_forward(2)

    take(8, 9)
    start(10, 11)
    swap(slot(3, 3)).start()
    swap(slot(3, 1)).start()
    row_forward(3)
    for a in range(8):
        front(a).wait()
    row_take(0)
    row_take(1)

    @pl.loop(0, 32)
    def _(i):
        @pl.when(i == 10)
        def _():
            take(12, 13)
            start(14, 15)
            swap(slot(1, 3)).start()
            swap(slot(1, 1)).start()
            row_take(2)
            row_take(3)

        @pl.when(i == 22)
        def _():
            take(16, 17)
            start(18, 19)
            swap(slot(2, 3)).start()
            swap(slot(2, 1)).start()

        for q in (1, 2, 3):

            @pl.when(i == 24 + 2 * q)
            def _():
                take(6 + 4 * q, 7 + 4 * q)
                swap(slot(Q_AT[q], 2)).start()

        other = i % 2
        e, f, g, h = i // 2, i // 2 - 5, i // 2 - 11, i // 2 - 13
        ahead = jnp.where(i < 26, 2, jnp.where(h == 0, 3, h))
        aside = jnp.where(i < 26, 1 + 2 * g, 2)
        turn = c + other * (1 - 2 * c)
        late_x, late_z = (1 - turn) * ahead + turn * aside, turn * ahead + (1 - turn) * aside
        near_x, near_z = jnp.where(e == 1, 2, 0), jnp.where(e >= 2, e - 1, 0)
        next_x, next_z = 1 + 2 * (f % 2), (f // 2) * (f // 2 + 1) // 2
        dx = jnp.where(i < 10, near_x, jnp.where(i < 22, next_x, late_x))
        dz = jnp.where(i < 10, near_z, jnp.where(i < 22, next_z, late_z))

        @pl.when((other == 1) & (i != 1) & (i != 11) & (i != 13))
        def _():
            take_swap(at(dx, dz))

        multiply(dx, dz, other)

    share.wait_send()
    if extra:

        @pl.when(c == 1)
        def _():
            give.wait_send()

    for k in range(20):
        copy(k).wait_send()

    @pl.loop(0, 16)
    def _(at_slot):
        swap(at_slot).wait_send()

    for j in range(4):

        @pl.when(place == 0)
        def _():
            row_copy(j, 1).wait_send()
            row_copy(j, -1).wait_send()

        @pl.when(place == 1)
        def _():
            row_relay(j).wait_send()


def pack(sizes_at, p_ref, o_ref, branch_at, panel, sizes_ref, branch_ref, sem):
    gz = lax.axis_index("gz")
    fetches = []
    for k in range(2):
        part = pl.ds(k * WIDTH, WIDTH)
        fetches.append(pltpu.make_async_copy(p_ref.at[:, part], panel.at[:, part], sem.at[k]))
        fetches[k].start()
    ask = pltpu.make_async_copy(sizes_at, sizes_ref, sem.at[2])
    ask.start()
    ask.wait()
    totals = [sum(sizes_ref[4 * k + i] for i in range(4)) for k in range(2)]
    need = jnp.maximum((jnp.maximum(totals[0], totals[1]) + 1 - EXTRA) // 2, (totals[0] + totals[1] + 3) // 4)
    branch, wide = 0, WIDES[0]
    for low, high in zip(WIDES[:-1], WIDES[1:]):
        over = (need > low).astype(jnp.int32)
        branch, wide = branch + over, wide + over * (high - low)
    branch_ref[0] = branch
    tell = pltpu.make_async_copy(branch_ref, branch_at, sem.at[3])
    tell.start()
    extra = EXTRA * (need <= WIDES[-2]).astype(jnp.int32)
    end = 2 * wide + extra
    sizes = [sizes_ref[2 * gz], sizes_ref[2 * gz + 1]]
    begin = jnp.where(gz == 0, 0, jnp.where(gz == 1, totals[0], end)) - jnp.where(gz == 3, totals[1], jnp.where(gz == 0, 0, sizes[0] + sizes[1]))
    begins = [begin, begin + sizes[0], begin + sizes[0] + sizes[1]]
    line = lax.broadcasted_iota(jnp.int32, (TILE, WINDOW), 0)
    shift = lax.broadcasted_iota(jnp.int32, (TILE, WINDOW), 1) - line

    @pl.loop(0, (end + TILE - 1) // TILE)
    def _(t):
        o_ref[pl.ds(pl.multiple_of(t * TILE, TILE), TILE)] = jnp.zeros((TILE, PIECE), jnp.bfloat16)

    for k in range(2):
        fetches[k].wait()

        def place(t, carry):
            ahead = t * TILE - begins[k]
            window = jnp.clip((ahead + 4 * WIDTH) // LANES * LANES - 4 * WIDTH, 0, WIDTH - WINDOW)
            pick = (shift == ahead - window) & (line < begins[k + 1] - t * TILE)
            part = panel[:, pl.ds(pl.multiple_of(k * WIDTH + window, LANES), WINDOW)]
            moved = lax.dot_general(
                pick.astype(jnp.bfloat16), part, (((1,), (1,)), ((), ())), preferred_element_type=jnp.float32
            ).astype(jnp.bfloat16)
            here = pl.ds(pl.multiple_of(t * TILE, TILE), TILE)
            o_ref[here] = o_ref[here] + moved
            return carry

        lax.fori_loop(begins[k] // TILE, (begins[k + 1] + TILE - 1) // TILE, place, 0)

    tell.wait()


def deliver(acc, o_ref, sem):
    moves = [pltpu.make_async_copy(acc.at[a], o_ref.at[:, pl.ds(a * PIECE, PIECE)], sem.at[a]) for a in range(8)]
    for move in moves:
        move.start()
    for move in moves:
        move.wait()


def update(wide, number, packed, front):
    extra = 0 if wide == 2 * WIDTH else EXTRA
    call = pl.pallas_call(
        functools.partial(kernel, wide),
        out_shape=pltpu.VMEM((8, PIECE, PIECE), jnp.float32),
        in_specs=[pl.BlockSpec(memory_space=pl.ANY)] * 2,
        out_specs=pl.BlockSpec(memory_space=pltpu.VMEM),
        scratch_shapes=[
            pltpu.VMEM((wide + extra, PIECE), jnp.bfloat16),
            pltpu.VMEM((max(extra, LANES), PIECE), jnp.bfloat16),
            pltpu.VMEM((max(extra, LANES), PIECE), jnp.bfloat16),
            pltpu.VMEM((2, 16, wide, PIECE), jnp.bfloat16),
            pltpu.VMEM((4, wide, PIECE), jnp.bfloat16),
            pltpu.SemaphoreType.DMA,
            pltpu.SemaphoreType.DMA,
            pltpu.SemaphoreType.DMA,
            pltpu.SemaphoreType.DMA,
            pltpu.SemaphoreType.DMA((20,)),
            pltpu.SemaphoreType.DMA((20,)),
            pltpu.SemaphoreType.DMA((16,)),
            pltpu.SemaphoreType.DMA((16,)),
            pltpu.SemaphoreType.DMA((4, 2)),
            pltpu.SemaphoreType.DMA((4,)),
            pltpu.SemaphoreType.DMA((6,)),
            pltpu.SemaphoreType.DMA((8,)),
        ],
        compiler_params=pltpu.CompilerParams(
            collective_id=number, has_side_effects=True, vmem_limit_bytes=PIECE * 2 * (37 * wide + 3 * max(extra, LANES)) + (2**20 if wide == 2 * WIDTH else 2**21)
        ),
    )
    return pl.pallas_call(
        deliver,
        out_shape=jax.ShapeDtypeStruct(front.shape, jnp.float32),
        in_specs=[pl.BlockSpec(memory_space=pltpu.VMEM)],
        out_specs=pl.BlockSpec(memory_space=pl.ANY),
        scratch_shapes=[pltpu.SemaphoreType.DMA((8,))],
        compiler_params=pltpu.CompilerParams(vmem_limit_bytes=2**20),
    )(call(packed, front))


def shards(panels, sizes, front):
    packed, branch = pl.pallas_call(
        pack,
        out_shape=[
            jax.ShapeDtypeStruct((4 * WIDTH, PIECE), jnp.bfloat16),
            jax.ShapeDtypeStruct((1,), jnp.int32),
        ],
        in_specs=[pl.BlockSpec(memory_space=pl.ANY)] * 2,
        out_specs=[pl.BlockSpec(memory_space=pltpu.VMEM), pl.BlockSpec(memory_space=pl.ANY)],
        scratch_shapes=[
            pltpu.VMEM((PIECE, 2 * WIDTH), jnp.bfloat16),
            pltpu.SMEM((8,), jnp.int32),
            pltpu.SMEM((1,), jnp.int32),
            pltpu.SemaphoreType.DMA((4,)),
        ],
    )(sizes, panels)
    calls = [functools.partial(update, wide, number) for number, wide in enumerate(WIDES)]
    return lax.switch(branch[0], calls, packed, front)


def solution(mesh):
    placed = (P(("gx", "gy"), "gz"), P(), P(("gx", "gz"), "gy"))
    return jax.shard_map(
        shards, mesh=mesh, in_specs=placed, out_specs=P(("gx", "gz"), "gy"), check_vma=False
    )
```

```python
import functools

import jax
import jax.numpy as jnp
from jax import lax
from jax.experimental import pallas as pl
from jax.experimental.pallas import tpu as pltpu
from jax.sharding import PartitionSpec as P

WIDTH = 1024
PIECE = 384
LANES = 128
STEP = 64
TILE = 256
WINDOW = TILE + LANES
MESH = pl.DeviceIdType.MESH
Q_AT = (0, 3, 1, 2)
WIDES = (704, 832, 896, 960, 1024, 1088, 1152, 1216, 1280, 1344, 1408, 1536, 1792, 2048)
EXTRA = 256


def device(x, y, z, c):
    return (x // 2) * 4 + z, y, (x % 2) * 2 + c


def kernel(wide, p_ref, f_ref, acc, stage, over, taken, cols, rows, r_send, r_recv, e_send, e_recv, i_send, i_recv, s_send, s_recv, x_send, x_recv, y_send, y_recv, l_sem, f_sem):
    gx, y, gz = lax.axis_index("gx"), lax.axis_index("gy"), lax.axis_index("gz")
    x_lo, c, z = gz // 2, gz % 2, gx % 4
    x = (gx // 4) * 2 + x_lo
    sign = 2 * c - 1

    def at(dx, dz):
        return ((x + dx) % 4) * 4 + (z + dz) % 4

    def slot(p, s):
        return at((1 - c) * p + c * s, c * p + (1 - c) * s)

    def along_p(d):
        return device((x + (1 - c) * d) % 4, y, (z + c * d) % 4, c)

    def along_s(d):
        return device((x + c * d) % 4, y, (z + (1 - c) * d) % 4, c)

    def along_y(d):
        return device(x, (y + 4 + d * sign) % 4, z, c)

    partner = device(x, y, z, 1 - c)
    whole, top, bottom = pl.ds(0, wide), pl.ds(0, wide // 2), pl.ds(wide // 2, wide // 2)

    def block(core, at_slot, part=whole):
        return cols.at[core, at_slot, part]

    def send(k, src, dst, to):
        return pltpu.make_async_remote_copy(src, dst, s_send.at[k], s_recv.at[k], device_id=to, device_id_type=MESH)

    def copy(k):
        if k < 2:
            return send(k, block(c, slot(0, 0)), block(c, slot(0, 0)), along_p(1 + 2 * k))
        if k < 4:
            ref = block(c, slot(3 if k == 2 else 1, 0), (top, bottom)[k - 2])
            return send(k, ref, ref, along_p(2 * k - 3))
        q, kind = k // 4 - 1, k % 4
        if kind < 2:
            here = block(c, slot(Q_AT[q], 0))
            return send(k, here, here, along_s(1 + 2 * kind))
        ref = block(c, slot(Q_AT[q], 3 if kind == 2 else 1), (top, bottom)[kind - 2])
        return send(k, ref, ref, along_s(2 * kind - 3))

    def arrival(k):
        if k < 4:
            where = (slot(3, 0), slot(1, 0), slot(2, 0), slot(2, 0))[k]
        else:
            p = Q_AT[(k - 4) // 4]
            where = (slot(p, 3), slot(p, 1), slot(p, 2), slot(p, 2))[k % 4]
        part = (whole, whole, top, bottom)[k % 4]
        ref = block(c, where, part)
        return send(k, ref, ref, partner)

    def start(*ks):
        for k in ks:
            copy(k).start()

    def take(*ks):
        for k in ks:
            arrival(k).wait_recv()

    def swap(at_slot):
        src = block(c, at_slot)
        return pltpu.make_async_remote_copy(
            src, block(c, at_slot), x_send.at[at_slot], x_recv.at[at_slot], device_id=partner, device_id_type=MESH
        )

    def take_swap(at_slot):
        ref = block(1 - c, at_slot)
        pltpu.make_async_remote_copy(
            ref, ref, x_send.at[at_slot], x_recv.at[at_slot], device_id=partner, device_id_type=MESH
        ).wait_recv()

    place = ((y - gz) * sign + 8) % 4
    beside = x + 1 - 2 * x_lo

    def row_src(j):
        return block(c if j % 2 == 0 else 1 - c, (beside if j >= 2 else x) * 4 + z)

    def row_copy(j, d):
        return pltpu.make_async_remote_copy(
            row_src(j), rows.at[j], y_send.at[j, 0 if d == 1 else 1], y_recv.at[j], device_id=along_y(d), device_id_type=MESH
        )

    def row_relay(j):
        return pltpu.make_async_remote_copy(
            rows.at[j], rows.at[j], y_send.at[j, 0], y_recv.at[j], device_id=along_y(1), device_id_type=MESH
        )

    def row_local(j):
        return pltpu.make_async_copy(row_src(j), rows.at[j], l_sem.at[j])

    def row_start(j):
        @pl.when(place == 0)
        def _():
            row_copy(j, 1).start()
            row_copy(j, -1).start()
            row_local(j).start()

    def row_forward(j):
        @pl.when(place == 1)
        def _():
            row_relay(j).wait_recv()
            row_relay(j).start()

    def row_take(j):
        @pl.when(place == 0)
        def _():
            row_local(j).wait()

        @pl.when(place >= 2)
        def _():
            row_relay(j).wait_recv()

    def front(a):
        return pltpu.make_async_copy(f_ref.at[:, pl.ds(a * PIECE, PIECE)], acc.at[a], f_sem.at[a])

    def multiply(dx, dz, other):
        xs, zs = (x + dx) % 4, (z + dz) % 4
        a = (xs // 2) * 4 + zs
        core = c + other * (1 - 2 * c)
        j = 2 * (dx % 2) + other

        acc[a] = acc[a] - lax.dot_general(
            rows[j], cols[core, xs * 4 + zs], (((0,), (0,)), ((), ())), preferred_element_type=jnp.float32
        )

    here = slot(0, 0)

    extra = 0 if wide == 2 * WIDTH else EXTRA
    mine_at, other_at = (x_lo + c) % 2 * wide, (x_lo + c + 1) % 2 * wide
    block_in, over_in = x_lo * extra, (1 - x_lo) * wide

    def columns(begin, count):
        return pl.ds(pl.multiple_of(begin, STEP), count)

    own = pltpu.make_async_copy(p_ref.at[columns(mine_at + block_in, wide)], block(c, here), l_sem.at[4])
    own.start()
    for a in range(8):
        front(a).start()
    barrier = pltpu.get_barrier_semaphore()
    near = [along_p(1), along_p(3), along_s(1), along_s(3), along_y(1), along_y(-1), partner]
    for to in near:
        pl.semaphore_signal(barrier, inc=1, device_id=to, device_id_type=MESH)
    pl.semaphore_wait(barrier, len(near))

    share = pltpu.make_async_remote_copy(
        p_ref.at[columns(other_at + block_in, wide)],
        stage.at[columns(block_in, wide)],
        r_send,
        r_recv,
        device_id=partner,
        device_id_type=MESH,
    )
    if extra:
        part = columns(over_in, extra)
        share_over = pltpu.make_async_remote_copy(
            p_ref.at[columns(other_at + over_in, extra)],
            stage.at[part],
            e_send,
            e_recv,
            device_id=partner,
            device_id_type=MESH,
        )
        give = pltpu.make_async_remote_copy(
            over, taken, i_send, i_recv, device_id=device(beside, y, z, c), device_id_type=MESH
        )
        spare = pltpu.make_async_copy(p_ref.at[columns(mine_at + over_in, extra)], over, l_sem.at[5])

        @pl.when(c == 0)
        def _():
            share_over.start()

        share.start()

        @pl.when(c == 1)
        def _():
            spare.start()
            spare.wait()
            share_over.wait_recv()
            over[...] = over[...] + stage[part]
            give.start()

    else:
        share.start()
    own.wait()
    share.wait_recv()

    @pl.loop(0, wide // STEP)
    def _(i):
        at_rows = columns(i * STEP, STEP)
        cols[c, here, at_rows] = cols[c, here, at_rows] + stage[columns(block_in + i * STEP, STEP)]

    if extra:

        @pl.when(c == 1)
        def _():
            give.wait_recv()
            took = columns((1 - x_lo) * (wide - extra), extra)
            cols[c, here, took] = cols[c, here, took] + taken[...]

    start(0, 1, 4, 5)
    swap(here).start()
    row_start(0)

    take_swap(here)
    row_start(1)
    row_forward(0)

    take(0, 1)
    start(2, 3)
    take(4, 5)
    start(6, 7, 8, 9, 12, 13)
    for p, s in ((3, 0), (1, 0), (0, 3), (0, 1)):
        swap(slot(p, s)).start()
    row_start(2)
    row_forward(1)
    take_swap(at(1, 0))
    take_swap(at(3, 0))
    row_start(3)

    take(2, 3)
    start(16, 17)
    swap(slot(2, 0)).start()
    take(6, 7)
    swap(slot(0, 2)).start()
    row_forward(2)

    take(8, 9)
    start(10, 11)
    swap(slot(3, 3)).start()
    swap(slot(3, 1)).start()
    row_forward(3)
    for a in range(8):
        front(a).wait()
    row_take(0)
    row_take(1)

    @pl.loop(0, 32)
    def _(i):
        @pl.when(i == 10)
        def _():
            take(12, 13)
            start(14, 15)
            swap(slot(1, 3)).start()
            swap(slot(1, 1)).start()
            row_take(2)
            row_take(3)

        @pl.when(i == 22)
        def _():
            take(16, 17)
            start(18, 19)
            swap(slot(2, 3)).start()
            swap(slot(2, 1)).start()

        for q in (1, 2, 3):

            @pl.when(i == 24 + 2 * q)
            def _():
                take(6 + 4 * q, 7 + 4 * q)
                swap(slot(Q_AT[q], 2)).start()

        other = i % 2
        e, f, g, h = i // 2, i // 2 - 5, i // 2 - 11, i // 2 - 13
        ahead = jnp.where(i < 26, 2, jnp.where(h == 0, 3, h))
        aside = jnp.where(i < 26, 1 + 2 * g, 2)
        turn = c + other * (1 - 2 * c)
        late_x, late_z = (1 - turn) * ahead + turn * aside, turn * ahead + (1 - turn) * aside
        near_x, near_z = jnp.where(e == 1, 2, 0), jnp.where(e >= 2, e - 1, 0)
        next_x, next_z = 1 + 2 * (f % 2), (f // 2) * (f // 2 + 1) // 2
        dx = jnp.where(i < 10, near_x, jnp.where(i < 22, next_x, late_x))
        dz = jnp.where(i < 10, near_z, jnp.where(i < 22, next_z, late_z))

        @pl.when((other == 1) & (i != 1) & (i != 11) & (i != 13))
        def _():
            take_swap(at(dx, dz))

        multiply(dx, dz, other)

    share.wait_send()
    if extra:

        @pl.when(c == 1)
        def _():
            give.wait_send()

        @pl.when(c == 0)
        def _():
            share_over.wait_send()

    for k in range(20):
        copy(k).wait_send()

    @pl.loop(0, 16)
    def _(at_slot):
        swap(at_slot).wait_send()

    for j in range(4):

        @pl.when(place == 0)
        def _():
            row_copy(j, 1).wait_send()
            row_copy(j, -1).wait_send()

        @pl.when(place == 1)
        def _():
            row_relay(j).wait_send()


def pack(sizes_at, p_ref, o_ref, branch_at, panel, sizes_ref, branch_ref, sem):
    gz = lax.axis_index("gz")
    fetches = []
    for k in range(2):
        part = pl.ds(k * WIDTH, WIDTH)
        fetches.append(pltpu.make_async_copy(p_ref.at[:, part], panel.at[:, part], sem.at[k]))
        fetches[k].start()
    ask = pltpu.make_async_copy(sizes_at, sizes_ref, sem.at[2])
    ask.start()
    ask.wait()
    totals = [sum(sizes_ref[4 * k + i] for i in range(4)) for k in range(2)]
    need = jnp.maximum((jnp.maximum(totals[0], totals[1]) + 1 - EXTRA) // 2, (totals[0] + totals[1] + 3) // 4)
    branch, wide = 0, WIDES[0]
    for low, high in zip(WIDES[:-1], WIDES[1:]):
        over = (need > low).astype(jnp.int32)
        branch, wide = branch + over, wide + over * (high - low)
    branch_ref[0] = branch
    tell = pltpu.make_async_copy(branch_ref, branch_at, sem.at[3])
    tell.start()
    extra = EXTRA * (need <= WIDES[-2]).astype(jnp.int32)
    end = 2 * wide + extra
    sizes = [sizes_ref[2 * gz], sizes_ref[2 * gz + 1]]
    begin = jnp.where(gz == 0, 0, jnp.where(gz == 1, totals[0], end)) - jnp.where(gz == 3, totals[1], jnp.where(gz == 0, 0, sizes[0] + sizes[1]))
    begins = [begin, begin + sizes[0], begin + sizes[0] + sizes[1]]
    line = lax.broadcasted_iota(jnp.int32, (TILE, WINDOW), 0)
    shift = lax.broadcasted_iota(jnp.int32, (TILE, WINDOW), 1) - line

    @pl.loop(0, (end + TILE - 1) // TILE)
    def _(t):
        o_ref[pl.ds(pl.multiple_of(t * TILE, TILE), TILE)] = jnp.zeros((TILE, PIECE), jnp.bfloat16)

    for k in range(2):
        fetches[k].wait()

        def place(t, carry):
            ahead = t * TILE - begins[k]
            window = jnp.clip((ahead + 4 * WIDTH) // LANES * LANES - 4 * WIDTH, 0, WIDTH - WINDOW)
            pick = (shift == ahead - window) & (line < begins[k + 1] - t * TILE)
            part = panel[:, pl.ds(pl.multiple_of(k * WIDTH + window, LANES), WINDOW)]
            moved = lax.dot_general(
                pick.astype(jnp.bfloat16), part, (((1,), (1,)), ((), ())), preferred_element_type=jnp.float32
            ).astype(jnp.bfloat16)
            here = pl.ds(pl.multiple_of(t * TILE, TILE), TILE)
            o_ref[here] = o_ref[here] + moved
            return carry

        lax.fori_loop(begins[k] // TILE, (begins[k + 1] + TILE - 1) // TILE, place, 0)

    tell.wait()


def deliver(acc, o_ref, sem):
    moves = [pltpu.make_async_copy(acc.at[a], o_ref.at[:, pl.ds(a * PIECE, PIECE)], sem.at[a]) for a in range(8)]
    for move in moves:
        move.start()
    for move in moves:
        move.wait()


def update(wide, number, packed, front):
    extra = 0 if wide == 2 * WIDTH else EXTRA
    call = pl.pallas_call(
        functools.partial(kernel, wide),
        out_shape=pltpu.VMEM((8, PIECE, PIECE), jnp.float32),
        in_specs=[pl.BlockSpec(memory_space=pl.ANY)] * 2,
        out_specs=pl.BlockSpec(memory_space=pltpu.VMEM),
        scratch_shapes=[
            pltpu.VMEM((wide + extra, PIECE), jnp.bfloat16),
            pltpu.VMEM((max(extra, LANES), PIECE), jnp.bfloat16),
            pltpu.VMEM((max(extra, LANES), PIECE), jnp.bfloat16),
            pltpu.VMEM((2, 16, wide, PIECE), jnp.bfloat16),
            pltpu.VMEM((4, wide, PIECE), jnp.bfloat16),
            pltpu.SemaphoreType.DMA,
            pltpu.SemaphoreType.DMA,
            pltpu.SemaphoreType.DMA,
            pltpu.SemaphoreType.DMA,
            pltpu.SemaphoreType.DMA,
            pltpu.SemaphoreType.DMA,
            pltpu.SemaphoreType.DMA((20,)),
            pltpu.SemaphoreType.DMA((20,)),
            pltpu.SemaphoreType.DMA((16,)),
            pltpu.SemaphoreType.DMA((16,)),
            pltpu.SemaphoreType.DMA((4, 2)),
            pltpu.SemaphoreType.DMA((4,)),
            pltpu.SemaphoreType.DMA((6,)),
            pltpu.SemaphoreType.DMA((8,)),
        ],
        compiler_params=pltpu.CompilerParams(
            collective_id=number, has_side_effects=True, vmem_limit_bytes=PIECE * 2 * (37 * wide + 3 * max(extra, LANES)) + (2**20 if wide == 2 * WIDTH else 2**21)
        ),
    )
    return pl.pallas_call(
        deliver,
        out_shape=jax.ShapeDtypeStruct(front.shape, jnp.float32),
        in_specs=[pl.BlockSpec(memory_space=pltpu.VMEM)],
        out_specs=pl.BlockSpec(memory_space=pl.ANY),
        scratch_shapes=[pltpu.SemaphoreType.DMA((8,))],
        compiler_params=pltpu.CompilerParams(vmem_limit_bytes=2**20),
    )(call(packed, front))


def shards(panels, sizes, front):
    packed, branch = pl.pallas_call(
        pack,
        out_shape=[
            jax.ShapeDtypeStruct((4 * WIDTH, PIECE), jnp.bfloat16),
            jax.ShapeDtypeStruct((1,), jnp.int32),
        ],
        in_specs=[pl.BlockSpec(memory_space=pl.ANY)] * 2,
        out_specs=[pl.BlockSpec(memory_space=pltpu.VMEM), pl.BlockSpec(memory_space=pl.ANY)],
        scratch_shapes=[
            pltpu.VMEM((PIECE, 2 * WIDTH), jnp.bfloat16),
            pltpu.SMEM((8,), jnp.int32),
            pltpu.SMEM((1,), jnp.int32),
            pltpu.SemaphoreType.DMA((4,)),
        ],
    )(sizes, panels)
    calls = [functools.partial(update, wide, number) for number, wide in enumerate(WIDES)]
    return lax.switch(branch[0], calls, packed, front)


def solution(mesh):
    placed = (P(("gx", "gy"), "gz"), P(), P(("gx", "gz"), "gy"))
    return jax.shard_map(
        shards, mesh=mesh, in_specs=placed, out_specs=P(("gx", "gz"), "gy"), check_vma=False
    )
```
